512 devices in a mesh: wide: 32 (over x, y), narrow: 16 (over z, core).
Axes of the slice: x: 4, y: 8, z: 8, core: 2. Of those that a mesh axis runs over, the one named last changes fastest.
Arguments:
- inverse: float32 [16384, 16384], P('wide', 'narrow'), may hold values from -0.2 to 1.3, as said below
- activations: bfloat16 [4096, 16384], P('narrow', 'wide'), may hold values from -4 to 4
- forget: int32 [512], replicated, may hold values from 0 to 4095, as said below
Outputs:
- downdated: float32 [16384, 16384], P('wide', 'narrow')
The draws below stay inside these ranges and needn't reach their ends.
Inputs may be any that keep to these rules, and one draw needn't show every extreme that they name: `inverse`: symmetric positive definite; the factor stays positive definite after every downdate. `forget`: distinct row numbers; rows are stored in order of arrival, and the newest one, 4095, whose request starts the downdate, is always among them.
All inputs are finite; a program needn't handle non-finite values.
Results may differ from the reference program's by a relative error of at most 0.0003.
Values may be sent and summed in bfloat16 or wider, within the bound.
No kernel may reach another device: no remote copies, remote signals or barrier semaphores. Data moves between devices by JAX's collectives and lax.ppermute only.
A program may use at most 64 MiB of HBM per device.

```python
import math
import jax
import jax.numpy as jnp
from jax import lax

M = 16384
GROUP = 256
GROUPS = 2
ROWS = 512
STORED = 4096


def draw_inverse(key, part):
    first, second = jax.random.split(key)
    spread = 0.2
    diag_lo = 0.9
    diag_hi = 1.1
    noise = jax.random.normal(first, (M, M), jnp.float32) * (spread / jnp.sqrt(2.0 * M))
    diagonal = jax.random.uniform(second, (M,), jnp.float32, diag_lo, diag_hi)
    places = jnp.arange(M)
    result = noise + noise.T
    result = jnp.where(places[:, None] == places[None, :], diagonal[None, :], result)
    return result


def draw_activations(key, part):
    values = jnp.clip(jax.random.normal(key, (STORED, M), jnp.float32), -4.0, 4.0)
    return values.astype(jnp.bfloat16)


def draw_forget(key, part):
    chosen = jax.random.permutation(jax.random.fold_in(key, 11), STORED - 1)[:ROWS - 1]
    joined = jnp.concatenate([chosen.astype(jnp.int32), jnp.full((1,), STORED - 1, jnp.int32)])
    return jax.random.permutation(jax.random.fold_in(key, 12), joined).astype(jnp.int32)


def setup_inputs(seed: int = 0) -> dict:
    seeds = jax.random.split(jax.random.key(seed), 4)
    return {
        "inverse": draw_inverse(jax.random.fold_in(seeds[3], 71), 0),
        "activations": draw_activations(jax.random.fold_in(seeds[3], 71), 0),
        "forget": draw_forget(jax.random.fold_in(seeds[3], 71), 0),
    }


def reference(inverse, activations, forget):
    current = inverse
    beta = 1.0 / (2.0 * (M + 4.0 * math.sqrt(ROWS * M)))
    for block_num in range(GROUPS):
        picked = forget[block_num * GROUP:(block_num + 1) * GROUP]
        block = jnp.take(activations, picked, axis=0).astype(jnp.float32)
        images = jnp.dot(block.astype(jnp.float32), current.astype(jnp.float32), precision=lax.Precision.HIGHEST, preferred_element_type=jnp.float32)
        capacity = jnp.dot(block.astype(jnp.float32), images.T.astype(jnp.float32), precision=lax.Precision.HIGHEST, preferred_element_type=jnp.float32)
        system = jnp.eye(GROUP, dtype=jnp.float32) / beta - capacity
        factor = jnp.linalg.cholesky(system)
        solved = jax.scipy.linalg.cho_solve((factor, True), images)
        current = current + jnp.dot(solved.T.astype(jnp.float32), images.astype(jnp.float32), precision=lax.Precision.HIGHEST, preferred_element_type=jnp.float32)
    return current
```

```python
import math

import jax
import jax.numpy as jnp
import numpy as np
from jax import lax
from jax.sharding import Mesh
from jax.sharding import PartitionSpec as P

M = 16384
ROWS = 512
BETA = 1.0 / (2.0 * (M + 4.0 * math.sqrt(ROWS * M)))
AXES = ("x", "y", "z", "core")
NX, NY, NZ, NC = 4, 8, 8, 2
F32 = jnp.float32
BF16 = jnp.bfloat16
SMALL = 2.0**-14
MAX_FACTORS = 48


def spread(x, axis, parts):
    x = x.reshape((parts, x.shape[0] // parts) + x.shape[1:])
    return lax.all_to_all(x, axis, 0, 0, tiled=True)


def scatter_sum(x, axis, parts):
    return jnp.sum(spread(x, axis, parts).astype(F32), axis=0)


def gather(x, axis, parts):
    got = lax.all_to_all(jnp.broadcast_to(x[None], (parts,) + x.shape), axis, 0, 0, tiled=True)
    return got.reshape((parts * x.shape[0],) + x.shape[1:])


def swap(x):
    return lax.ppermute(x, "core", [(0, 1), (1, 0)])


def fold_cores(x):
    core = lax.axis_index("core")
    half = x.shape[0] // 2
    there = lax.dynamic_slice_in_dim(x, (1 - core) * half, half, 0)
    here = lax.dynamic_slice_in_dim(x, core * half, half, 0)
    return here + swap(there)


def join_cores(x):
    other = swap(x)
    first = lax.axis_index("core") == 0
    return jnp.concatenate([jnp.where(first, x, other), jnp.where(first, other, x)], axis=0)


def exact_pair(x):
    high = lax.reduce_precision(x, 8, 7)
    return high.astype(BF16), (x - high).astype(BF16)


def column_owner():
    pairs = []
    for x in range(NX):
        for y in range(NY):
            for z in range(NZ):
                for core in range(NC):
                    here = ((x * NY + y) * NZ + z) * NC + core
                    to_x, to_y = 2 * (y % 2) + core, z
                    to_z, to_core = 2 * x + y // 4, (y // 2) % 2
                    pairs.append((here, ((to_x * NY + to_y) * NZ + to_z) * NC + to_core))
    return pairs


def solve_rows(start, square):
    def dot(a, b):
        return jnp.dot(a, b, precision=lax.Precision.HIGHEST, preferred_element_type=F32)

    def more(state):
        _, power, last, count = state
        return jnp.logical_and(last > SMALL, count < MAX_FACTORS)

    def step(state):
        total, power, _, count = state
        power = dot(power, power)
        return total + dot(total, power), power, jnp.max(jnp.sum(jnp.abs(power), axis=0)), count + 1

    state = (start + dot(start, square), square, jnp.float32(1.0), jnp.int32(0))
    return lax.while_loop(more, step, state)[0]


def on_device(inverse, activations, forget):
    x, y = lax.axis_index("x"), lax.axis_index("y")
    z, core = lax.axis_index("z"), lax.axis_index("core")
    wide, narrow = x * NY + y, z * NC + core
    height, width = inverse.shape
    stored_here = activations.shape[0]
    to_columns = column_owner()
    to_rows = [(b, a) for a, b in to_columns]

    local = forget - narrow * stored_here
    onehot = (jnp.arange(stored_here, dtype=jnp.int32)[:, None] == local[None, :]).astype(BF16)
    picked = lax.dot_general(
        activations, onehot, (((0,), (0,)), ((), ())), preferred_element_type=F32
    ).astype(BF16)
    piece = scatter_sum(fold_cores(picked), "z", NZ).astype(BF16)
    piece_by_columns = lax.ppermute(piece, AXES, to_columns)
    rows_here = join_cores(gather(piece, "z", NZ))

    row_number = wide * height + lax.broadcasted_iota(jnp.int32, inverse.shape, 0)
    col_number = narrow * width + lax.broadcasted_iota(jnp.int32, inverse.shape, 1)
    less_one = inverse - jnp.where(row_number == col_number, 1.0, 0.0).astype(F32)
    part = sum(
        lax.dot_general(term, rows_here, (((0,), (0,)), ((), ())), preferred_element_type=F32)
        for term in exact_pair(less_one)
    )
    summed = scatter_sum(part.astype(BF16), "x", NX)
    change = scatter_sum(summed.astype(BF16), "y", NY)
    images_piece = change + piece_by_columns.astype(F32)

    share = lax.dot_general(
        piece_by_columns.astype(F32),
        images_piece * BETA,
        (((0,), (0,)), ((), ())),
        precision=lax.Precision.HIGHEST,
        preferred_element_type=F32,
    )
    share = scatter_sum(fold_cores(share).astype(BF16), "z", NZ)
    share = scatter_sum(share, "y", NY)
    share = jnp.sum(gather(share[None], "x", NX), axis=0)
    scaled = join_cores(gather(gather(share, "y", NY), "z", NZ))

    change_here = join_cores(gather(lax.ppermute(change.astype(BF16), AXES, to_rows), "z", NZ))
    images_rows = rows_here.astype(F32) + change_here.astype(F32)
    images_cols = gather(gather(images_piece.astype(BF16), "y", NY), "x", NX)

    solved = solve_rows(images_rows * BETA, scaled)
    update = sum(
        lax.dot_general(term, images_cols, (((1,), (1,)), ((), ())), preferred_element_type=F32)
        for term in exact_pair(solved)
    )
    return inverse + update


def solution(mesh):
    devices = np.asarray(mesh.devices).reshape(NX, NY, NZ, NC)
    placed = (P(("x", "y"), ("z", "core")), P(("z", "core"), ("x", "y")), P())
    return jax.shard_map(
        on_device,
        mesh=Mesh(devices, AXES),
        in_specs=placed,
        out_specs=P(("x", "y"), ("z", "core")),
        check_vma=False,
    )
```

```python
import math

import jax
import jax.numpy as jnp
import numpy as np
from jax import lax
from jax.experimental.layout import Layout, with_layout_constraint
from jax.sharding import Mesh
from jax.sharding import PartitionSpec as P

M = 16384
ROWS = 512
BETA = 1.0 / (2.0 * (M + 4.0 * math.sqrt(ROWS * M)))
AXES = ("x", "y", "z", "core")
NX, NY, NZ, NC = 4, 8, 8, 2
F32 = jnp.float32
BF16 = jnp.bfloat16
SMALL = 2.0**-1.5
MAX_FACTORS = 48


def spread(x, axis, parts):
    x = x.reshape((parts, x.shape[0] // parts) + x.shape[1:])
    return lax.all_to_all(x, axis, 0, 0, tiled=True)


def scatter_sum(x, axis, parts):
    return jnp.sum(spread(x, axis, parts).astype(F32), axis=0)


def gather(x, axis, parts):
    got = lax.all_to_all(jnp.broadcast_to(x[None], (parts,) + x.shape), axis, 0, 0, tiled=True)
    return got.reshape((parts * x.shape[0],) + x.shape[1:])


def swap(x):
    return lax.ppermute(x, "core", [(0, 1), (1, 0)])


def fold_cores(x):
    core = lax.axis_index("core")
    half = x.shape[0] // 2
    there = lax.dynamic_slice_in_dim(x, (1 - core) * half, half, 0)
    here = lax.dynamic_slice_in_dim(x, core * half, half, 0)
    return here + swap(there)


def join_cores(x):
    other = swap(x)
    first = lax.axis_index("core") == 0
    return jnp.concatenate([jnp.where(first, x, other), jnp.where(first, other, x)], axis=0)


def exact_pair(x):
    high = lax.reduce_precision(x, 8, 7)
    return high.astype(BF16), (x - high).astype(BF16)


def column_owner():
    pairs = []
    for x in range(NX):
        for y in range(NY):
            for z in range(NZ):
                for core in range(NC):
                    here = ((x * NY + y) * NZ + z) * NC + core
                    to_x, to_y = 2 * (y % 2) + core, z
                    to_z, to_core = 2 * x + y // 4, (y // 2) % 2
                    pairs.append((here, ((to_x * NY + to_y) * NZ + to_z) * NC + to_core))
    return pairs


def solve_rows(start, square):
    def dot(a, b, precision=lax.Precision.HIGHEST):
        return jnp.dot(a, b, precision=precision, preferred_element_type=F32)

    def norm(power):
        return jnp.max(jnp.sum(jnp.abs(power), axis=0))

    def more(state):
        return jnp.logical_and(state[2] > SMALL, state[3] < MAX_FACTORS)

    def step(state):
        total, power, _, count = state
        power = dot(power, power)
        total = with_layout_constraint(total + dot(total, power), Layout((0, 1)))
        return total, power, norm(power), count + 1

    total, power = start + dot(start, square), square
    for _ in range(2):
        power = dot(power, power)
        total = total + dot(total, power)
    total, power, _, _ = lax.while_loop(more, step, (total, power, norm(power), jnp.int32(0)))
    for precision in (lax.Precision.HIGH, lax.Precision.HIGH, lax.Precision.DEFAULT):
        power = dot(power, power, precision)
        total = total + dot(total, power, precision)
    return total


def on_device(inverse, activations, forget):
    x, y = lax.axis_index("x"), lax.axis_index("y")
    z, core = lax.axis_index("z"), lax.axis_index("core")
    wide, narrow = x * NY + y, z * NC + core
    height, width = inverse.shape
    stored_here = activations.shape[0]
    to_columns = column_owner()
    to_rows = [(b, a) for a, b in to_columns]

    local = forget - narrow * stored_here
    onehot = (jnp.arange(stored_here, dtype=jnp.int32)[:, None] == local[None, :]).astype(BF16)
    picked = lax.dot_general(
        activations, onehot, (((0,), (0,)), ((), ())), preferred_element_type=F32
    ).astype(BF16)
    piece = scatter_sum(fold_cores(picked), "z", NZ).astype(BF16)
    piece_by_columns = lax.ppermute(piece, AXES, to_columns)
    rows_here = join_cores(gather(piece, "z", NZ))

    row_number = wide * height + lax.broadcasted_iota(jnp.int32, inverse.shape, 0)
    col_number = narrow * width + lax.broadcasted_iota(jnp.int32, inverse.shape, 1)
    less_one = inverse - jnp.where(row_number == col_number, 1.0, 0.0).astype(F32)
    part = sum(
        lax.dot_general(term, rows_here, (((0,), (0,)), ((), ())), preferred_element_type=F32)
        for term in exact_pair(less_one)
    )
    summed = scatter_sum(part.astype(BF16), "x", NX)
    change = scatter_sum(summed.astype(BF16), "y", NY)
    change = change.astype(BF16)
    both = jnp.concatenate([piece_by_columns, change], axis=0)
    both = gather(both, "y", NY).reshape(NY, 2, -1, both.shape[1])
    rows_cols = both[:, 0].reshape(-1, both.shape[3])
    change_cols = both[:, 1].reshape(-1, both.shape[3])

    share = sum(
        lax.dot_general(rows_cols, term, (((0,), (0,)), ((), ())), preferred_element_type=F32)
        for term in (rows_cols, change_cols)
    )
    share = scatter_sum(fold_cores(share * BETA).astype(BF16), "z", NZ)
    share = jnp.sum(gather(share[None], "x", NX), axis=0)

    change_there = lax.ppermute(change, AXES, to_rows)
    gathered = gather(jnp.concatenate(exact_pair(share) + (change_there,), axis=0), "z", NZ)
    mine, other = gathered, swap(gathered)
    first = core == 0
    halves = [jnp.where(first, mine, other), jnp.where(first, other, mine)]
    halves = [h.reshape(NZ, -1, h.shape[1]).astype(F32) for h in halves]
    n = share.shape[0]
    scaled = [(h[:, :n] + h[:, n : 2 * n]).reshape(-1, h.shape[2]) for h in halves]
    scaled = jnp.concatenate(scaled, axis=0)
    change_here = [h[:, 2 * n :].reshape(-1, h.shape[2]) for h in halves]
    change_here = jnp.concatenate(change_here, axis=0)
    images_rows = rows_here.astype(F32) + change_here
    images_cols = gather((rows_cols.astype(F32) + change_cols.astype(F32)).astype(BF16), "x", NX)

    solved = solve_rows(images_rows * BETA, scaled)
    update = sum(
        lax.dot_general(term, images_cols, (((1,), (1,)), ((), ())), preferred_element_type=F32)
        for term in exact_pair(solved)
    )
    return inverse + update


def solution(mesh):
    devices = np.asarray(mesh.devices).reshape(NX, NY, NZ, NC)
    placed = (P(("x", "y"), ("z", "core")), P(("z", "core"), ("x", "y")), P())
    return jax.shard_map(
        on_device,
        mesh=Mesh(devices, AXES),
        in_specs=placed,
        out_specs=P(("x", "y"), ("z", "core")),
        check_vma=False,
    )
```

```python
import math

import jax
import jax.numpy as jnp
import numpy as np
from jax import lax
from jax.experimental import pallas as pl
from jax.experimental.pallas import tpu as pltpu
from jax.experimental.layout import Layout, with_layout_constraint
from jax.sharding import Mesh
from jax.sharding import PartitionSpec as P


M = 16384
ROWS = 512
BETA = 1.0 / (2.0 * (M + 4.0 * math.sqrt(ROWS * M)))
AXES = ("x", "y", "z", "core")
NX, NY, NZ, NC = 4, 8, 8, 2
F32 = jnp.float32
BF16 = jnp.bfloat16
SMALL = 2.0**-1.5
MAX_FACTORS = 48
PAD = 8


def spread(x, axis, parts):
    x = x.reshape((parts, x.shape[0] // parts) + x.shape[1:])
    return lax.all_to_all(x, axis, 0, 0, tiled=True)


def scatter_sum(x, axis, parts):
    return jnp.sum(spread(x, axis, parts).astype(F32), axis=0)


def gather(x, axis, parts):
    got = lax.all_to_all(jnp.broadcast_to(x[None], (parts,) + x.shape), axis, 0, 0, tiled=True)
    return got.reshape((parts * x.shape[0],) + x.shape[1:])


def swap(x):
    return lax.ppermute(x, "core", [(0, 1), (1, 0)])


def fold_cores(x):
    core = lax.axis_index("core")
    half = x.shape[0] // 2
    there = lax.dynamic_slice_in_dim(x, (1 - core) * half, half, 0)
    here = lax.dynamic_slice_in_dim(x, core * half, half, 0)
    return here + swap(there)


def exact_pair(x):
    high = lax.reduce_precision(x, 8, 7)
    return high.astype(BF16), (x - high).astype(BF16)


def column_owner():
    pairs = []
    for x in range(NX):
        for y in range(NY):
            for z in range(NZ):
                for core in range(NC):
                    here = ((x * NY + y) * NZ + z) * NC + core
                    to_x, to_y = 2 * (y % 2) + core, z
                    to_z, to_core = 2 * x + y // 4, (y // 2) % 2
                    pairs.append((here, ((to_x * NY + to_y) * NZ + to_z) * NC + to_core))
    return pairs


def solve_rows(start, square):
    def dot(a, b, precision=lax.Precision.HIGH):
        return jnp.dot(a, b, precision=precision, preferred_element_type=F32)

    def norm(power):
        return jnp.max(jnp.sum(jnp.abs(power), axis=0))

    def more(state):
        return jnp.logical_and(state[2] > SMALL, state[3] < MAX_FACTORS)

    def step(state):
        total, power, _, count = state
        power = dot(power, power)
        total = with_layout_constraint(total + dot(total, power), Layout((0, 1)))
        return total, power, norm(power), count + 1

    total, power = start + dot(start, square), square
    for _ in range(2):
        power = dot(power, power)
        total = total + dot(total, power)
    total, power, _, _ = lax.while_loop(more, step, (total, power, norm(power), jnp.int32(0)))
    for precision in (lax.Precision.HIGH, lax.Precision.DEFAULT, lax.Precision.DEFAULT):
        power = dot(power, power, precision)
        total = total + dot(total, power, precision)
    return total


def add_product(inverse, solved, images):
    height, width = inverse.shape
    rows = solved.shape[1]
    block = height // 4

    def kernel(inverse_ref, solved_ref, images_ref, out_ref):
        left = solved_ref[...]
        high = left.astype(BF16)
        low = (left - high.astype(F32)).astype(BF16)
        total = inverse_ref[...]
        for term in (low, high):
            total += lax.dot_general(
                term, images_ref[...], (((1,), (1,)), ((), ())), preferred_element_type=F32
            )
        out_ref[...] = total

    return pl.pallas_call(
        kernel,
        out_shape=jax.ShapeDtypeStruct(inverse.shape, F32),
        grid=(height // block,),
        in_specs=[
            pl.BlockSpec((block, width), lambda i: (i, 0)),
            pl.BlockSpec((block, rows), lambda i: (i, 0)),
            pl.BlockSpec((width, rows), lambda i: (0, 0)),
        ],
        out_specs=pl.BlockSpec((block, width), lambda i: (i, 0)),
        cost_estimate=pl.CostEstimate(
            flops=4 * height * width * rows,
            bytes_accessed=8 * height * width + 4 * height * rows + 2 * width * rows,
            transcendentals=0,
        ),
        compiler_params=pltpu.CompilerParams(vmem_limit_bytes=61 << 20),
        name="add_product",
    )(inverse, solved, images)


def on_device(inverse, activations, forget):
    x, y = lax.axis_index("x"), lax.axis_index("y")
    z, core = lax.axis_index("z"), lax.axis_index("core")
    wide, narrow = x * NY + y, z * NC + core
    height, width = inverse.shape
    stored_here = activations.shape[0]
    to_columns = column_owner()
    to_rows = [(b, a) for a, b in to_columns]

    local = forget - narrow * stored_here
    onehot = (jnp.arange(stored_here, dtype=jnp.int32)[:, None] == local[None, :]).astype(BF16)
    picked = lax.dot_general(
        activations, onehot, (((0,), (0,)), ((), ())), preferred_element_type=F32
    ).astype(BF16)
    piece = scatter_sum(fold_cores(picked), "z", NZ).astype(BF16)
    half = gather(piece, "z", NZ)
    rows_cols = lax.ppermute(half, AXES, to_columns)
    rows_here = lax.all_gather(half, "core", axis=0, tiled=True)

    row_number = wide * height + lax.broadcasted_iota(jnp.int32, inverse.shape, 0)
    col_number = narrow * width + lax.broadcasted_iota(jnp.int32, inverse.shape, 1)
    less_one = inverse - jnp.where(row_number == col_number, 1.0, 0.0).astype(F32)
    part = sum(
        lax.dot_general(term, rows_here, (((0,), (0,)), ((), ())), preferred_element_type=F32)
        for term in exact_pair(less_one)
    )
    summed = scatter_sum(part.astype(BF16), "x", NX)
    change = scatter_sum(summed.astype(BF16), "y", NY)
    change = change.astype(BF16)
    change_cols = gather(change, "y", NY)

    share = sum(
        lax.dot_general(rows_cols, term, (((0,), (0,)), ((), ())), preferred_element_type=F32)
        for term in (rows_cols, change_cols)
    )
    share = scatter_sum(fold_cores(share * BETA).astype(BF16), "z", NZ)
    share = jnp.sum(gather(share[None], "x", NX), axis=0)

    n = share.shape[0]
    own = (core * NZ + z) * n + lax.broadcasted_iota(jnp.int32, share.shape, 0)
    on_diagonal = own == lax.broadcasted_iota(jnp.int32, share.shape, 1)
    high, low = exact_pair(share)
    low = jnp.sum(jnp.where(on_diagonal, low.astype(F32), 0.0), axis=0, keepdims=True)
    low = jnp.pad(low, ((0, PAD - 1), (0, 0))).astype(BF16)
    change_there = lax.ppermute(change, AXES, to_rows)
    gathered = gather(jnp.concatenate([high, low, change_there], axis=0), "z", NZ)
    mine, other = gathered, swap(gathered)
    first = core == 0
    halves = [jnp.where(first, mine, other), jnp.where(first, other, mine)]
    halves = [h.reshape(NZ, -1, h.shape[1]).astype(F32) for h in halves]
    scaled = jnp.concatenate([h[:, :n].reshape(-1, h.shape[2]) for h in halves], axis=0)
    low = jnp.sum(halves[0][:, n] + halves[1][:, n], axis=0)
    diagonal = lax.broadcasted_iota(jnp.int32, scaled.shape, 0) == lax.broadcasted_iota(
        jnp.int32, scaled.shape, 1
    )
    scaled = scaled + jnp.where(diagonal, low[None], 0.0)
    change_here = [h[:, n + PAD :].reshape(-1, h.shape[2]) for h in halves]
    change_here = jnp.concatenate(change_here, axis=0)
    images_rows = rows_here.astype(F32) + change_here
    images_cols = gather((rows_cols.astype(F32) + change_cols.astype(F32)).astype(BF16), "x", NX)

    solved = solve_rows(images_rows * BETA, scaled)
    return add_product(inverse, solved, images_cols)


def solution(mesh):
    devices = np.asarray(mesh.devices).reshape(NX, NY, NZ, NC)
    placed = (P(("x", "y"), ("z", "core")), P(("z", "core"), ("x", "y")), P())

    return jax.shard_map(
        on_device,
        mesh=Mesh(devices, AXES),
        in_specs=placed,
        out_specs=P(("x", "y"), ("z", "core")),
        check_vma=False,
    )
```

```python
import math

import jax
import jax.numpy as jnp
import numpy as np
from jax import lax
from jax.experimental.layout import Layout, with_layout_constraint
from jax.sharding import Mesh
from jax.sharding import PartitionSpec as P

M = 16384
ROWS = 512
BETA = 1.0 / (2.0 * (M + 4.0 * math.sqrt(ROWS * M)))
AXES = ("x", "y", "z", "core")
NX, NY, NZ, NC = 4, 8, 8, 2
F32 = jnp.float32
BF16 = jnp.bfloat16
SMALL = 2.0**-1.5
MAX_FACTORS = 48
PAD = 8


def spread(x, axis, parts):
    x = x.reshape((parts, x.shape[0] // parts) + x.shape[1:])
    return lax.all_to_all(x, axis, 0, 0, tiled=True)


def scatter_sum(x, axis, parts):
    return jnp.sum(spread(x, axis, parts).astype(F32), axis=0)


def gather(x, axis, parts):
    got = lax.all_to_all(jnp.broadcast_to(x[None], (parts,) + x.shape), axis, 0, 0, tiled=True)
    return got.reshape((parts * x.shape[0],) + x.shape[1:])


def swap(x):
    return lax.ppermute(x, "core", [(0, 1), (1, 0)])


def fold_cores(x):
    core = lax.axis_index("core")
    half = x.shape[0] // 2
    there = lax.dynamic_slice_in_dim(x, (1 - core) * half, half, 0)
    here = lax.dynamic_slice_in_dim(x, core * half, half, 0)
    return here + swap(there)


def join_cores(x):
    other = swap(x)
    first = lax.axis_index("core") == 0
    return jnp.concatenate([jnp.where(first, x, other), jnp.where(first, other, x)], axis=0)


def exact_pair(x):
    high = lax.reduce_precision(x, 8, 7)
    return high.astype(BF16), (x - high).astype(BF16)


def column_owner():
    pairs = []
    for x in range(NX):
        for y in range(NY):
            for z in range(NZ):
                for core in range(NC):
                    here = ((x * NY + y) * NZ + z) * NC + core
                    to_x, to_y = 2 * (y % 2) + core, z
                    to_z, to_core = 2 * x + y // 4, (y // 2) % 2
                    pairs.append((here, ((to_x * NY + to_y) * NZ + to_z) * NC + to_core))
    return pairs


def solve_rows(start, square):
    def dot(a, b, precision=lax.Precision.HIGH):
        return jnp.dot(a, b, precision=precision, preferred_element_type=F32)

    def norm(power):
        return jnp.max(jnp.sum(jnp.abs(power), axis=0))

    def more(state):
        return jnp.logical_and(state[2] > SMALL, state[3] < MAX_FACTORS)

    def step(state):
        total, power, _, count = state
        power = dot(power, power)
        total = with_layout_constraint(total + dot(total, power), Layout((0, 1)))
        return total, power, norm(power), count + 1

    total, power = start + dot(start, square), square
    for _ in range(2):
        power = dot(power, power)
        total = total + dot(total, power)
    total, power, _, _ = lax.while_loop(more, step, (total, power, norm(power), jnp.int32(0)))
    for precision in (lax.Precision.HIGH, lax.Precision.DEFAULT, lax.Precision.DEFAULT):
        power = dot(power, power, precision)
        total = total + dot(total, power, precision)
    return total


def on_device(inverse, activations, forget):
    x, y = lax.axis_index("x"), lax.axis_index("y")
    z, core = lax.axis_index("z"), lax.axis_index("core")
    wide, narrow = x * NY + y, z * NC + core
    height, width = inverse.shape
    stored_here = activations.shape[0]
    to_columns = column_owner()
    to_rows = [(b, a) for a, b in to_columns]

    local = forget - narrow * stored_here
    onehot = (jnp.arange(stored_here, dtype=jnp.int32)[:, None] == local[None, :]).astype(BF16)
    picked = lax.dot_general(
        activations, onehot, (((0,), (0,)), ((), ())), preferred_element_type=F32
    ).astype(BF16)
    piece = scatter_sum(fold_cores(picked), "z", NZ).astype(BF16)
    half = gather(piece, "z", NZ)
    piece_by_columns = lax.ppermute(piece, AXES, to_columns)
    rows_here = lax.all_gather(half, "core", axis=0, tiled=True)

    row_number = wide * height + lax.broadcasted_iota(jnp.int32, inverse.shape, 0)
    col_number = narrow * width + lax.broadcasted_iota(jnp.int32, inverse.shape, 1)
    less_one = inverse - jnp.where(row_number == col_number, 1.0, 0.0).astype(F32)
    part = sum(
        lax.dot_general(term, rows_here, (((0,), (0,)), ((), ())), preferred_element_type=F32)
        for term in exact_pair(less_one)
    )
    summed = scatter_sum(part.astype(BF16), "x", NX)
    change = scatter_sum(summed.astype(BF16), "y", NY)
    change = change.astype(BF16)
    both = jnp.concatenate([piece_by_columns, change], axis=0)
    both = gather(both, "y", NY).reshape(NY, 2, -1, both.shape[1])
    rows_cols = both[:, 0].reshape(-1, both.shape[3])
    change_cols = both[:, 1].reshape(-1, both.shape[3])

    share = sum(
        lax.dot_general(rows_cols, term, (((0,), (0,)), ((), ())), preferred_element_type=F32)
        for term in (rows_cols, change_cols)
    )
    share = scatter_sum(fold_cores(share * BETA).astype(BF16), "z", NZ)
    share = jnp.sum(gather(share[None], "x", NX), axis=0)

    n = share.shape[0]
    own = (core * NZ + z) * n + lax.broadcasted_iota(jnp.int32, share.shape, 0)
    on_diagonal = own == lax.broadcasted_iota(jnp.int32, share.shape, 1)
    high, low = exact_pair(share)
    low = jnp.sum(jnp.where(on_diagonal, low.astype(F32), 0.0), axis=0, keepdims=True)
    low = jnp.pad(low, ((0, PAD - 1), (0, 0))).astype(BF16)
    change_there = lax.ppermute(change, AXES, to_rows)
    gathered = gather(jnp.concatenate([high, low, change_there], axis=0), "z", NZ)
    mine, other = gathered, swap(gathered)
    first = core == 0
    halves = [jnp.where(first, mine, other), jnp.where(first, other, mine)]
    halves = [h.reshape(NZ, -1, h.shape[1]).astype(F32) for h in halves]
    scaled = jnp.concatenate([h[:, :n].reshape(-1, h.shape[2]) for h in halves], axis=0)
    low = jnp.sum(halves[0][:, n] + halves[1][:, n], axis=0)
    diagonal = lax.broadcasted_iota(jnp.int32, scaled.shape, 0) == lax.broadcasted_iota(
        jnp.int32, scaled.shape, 1
    )
    scaled = scaled + jnp.where(diagonal, low[None], 0.0)
    change_here = [h[:, n + PAD :].reshape(-1, h.shape[2]) for h in halves]
    change_here = jnp.concatenate(change_here, axis=0)
    images_rows = rows_here.astype(F32) + change_here
    images_cols = gather((rows_cols.astype(F32) + change_cols.astype(F32)).astype(BF16), "x", NX)

    solved = solve_rows(images_rows * BETA, scaled)
    return inverse + lax.dot_general(
        solved,
        images_cols.astype(F32),
        (((1,), (1,)), ((), ())),
        precision=lax.Precision.HIGH,
        preferred_element_type=F32,
    )


def solution(mesh):
    devices = np.asarray(mesh.devices).reshape(NX, NY, NZ, NC)
    placed = (P(("x", "y"), ("z", "core")), P(("z", "core"), ("x", "y")), P())
    return jax.shard_map(
        on_device,
        mesh=Mesh(devices, AXES),
        in_specs=placed,
        out_specs=P(("x", "y"), ("z", "core")),
        check_vma=False,
    )
```

```python
import math

import jax
import jax.numpy as jnp
import numpy as np
from jax import lax
from jax.experimental.layout import Layout, with_layout_constraint
from jax.sharding import Mesh
from jax.sharding import PartitionSpec as P

M = 16384
ROWS = 512
BETA = 1.0 / (2.0 * (M + 4.0 * math.sqrt(ROWS * M)))
AXES = ("x", "y", "z", "core")
NX, NY, NZ, NC = 4, 8, 8, 2
F32 = jnp.float32
BF16 = jnp.bfloat16
SMALL = 2.0**-6
MAX_FACTORS = 48
PAD = 8
SLOTS = 96


def spread(x, axis, parts):
    x = x.reshape((parts, x.shape[0] // parts) + x.shape[1:])
    return lax.all_to_all(x, axis, 0, 0, tiled=True)


def scatter_sum(x, axis, parts):
    return jnp.sum(spread(x, axis, parts).astype(F32), axis=0)


def gather(x, axis, parts):
    got = lax.all_to_all(jnp.broadcast_to(x[None], (parts,) + x.shape), axis, 0, 0, tiled=True)
    return got.reshape((parts * x.shape[0],) + x.shape[1:])


def swap(x):
    return lax.ppermute(x, "core", [(0, 1), (1, 0)])


def fold_cores(x):
    core = lax.axis_index("core")
    half = x.shape[0] // 2
    there = lax.dynamic_slice_in_dim(x, (1 - core) * half, half, 0)
    here = lax.dynamic_slice_in_dim(x, core * half, half, 0)
    return here + swap(there)


def join_cores(x):
    other = swap(x)
    first = lax.axis_index("core") == 0
    return jnp.concatenate([jnp.where(first, x, other), jnp.where(first, other, x)], axis=0)


def exact_pair(x):
    high = lax.reduce_precision(x, 8, 7)
    return high.astype(BF16), (x - high).astype(BF16)


def column_owner():
    pairs = []
    for x in range(NX):
        for y in range(NY):
            for z in range(NZ):
                for core in range(NC):
                    here = ((x * NY + y) * NZ + z) * NC + core
                    to_x, to_y = 2 * (y % 2) + core, z
                    to_z, to_core = 2 * x + y // 4, (y // 2) % 2
                    pairs.append((here, ((to_x * NY + to_y) * NZ + to_z) * NC + to_core))
    return pairs


def solve_rows(start, square):
    def dot(a, b, precision=lax.Precision.HIGH):
        return jnp.dot(a, b, precision=precision, preferred_element_type=F32)

    def norm(power):
        return jnp.max(jnp.sum(jnp.abs(power), axis=0))

    def more(state):
        return jnp.logical_and(state[2] > SMALL, state[3] < MAX_FACTORS)

    def step(state):
        total, power, _, count = state
        power = dot(power, power)
        total = with_layout_constraint(total + dot(total, power), Layout((0, 1)))
        return total, power, norm(power), count + 1

    total, power = start + dot(start, square), square
    for _ in range(3):
        power = dot(power, power)
        total = total + dot(total, power)
    total, power, _, _ = lax.while_loop(more, step, (total, power, norm(power), jnp.int32(0)))
    power = dot(power, power, lax.Precision.DEFAULT)
    total = total + dot(total, power, lax.Precision.DEFAULT)
    return total


def forgotten_half(activations, forget):
    z, core = lax.axis_index("z"), lax.axis_index("core")
    stored_here, features = activations.shape
    rows = forget.shape[0]
    first_here = (z * NC + core) * stored_here
    chip = forget // (NC * stored_here)

    earlier = lax.broadcasted_iota(jnp.int32, (rows, rows), 0) < lax.broadcasted_iota(
        jnp.int32, (rows, rows), 1
    )
    rank = jnp.sum((earlier & (chip[:, None] == chip[None, :])).astype(jnp.int32), axis=0)

    def onehot(places, numbers):
        return (jnp.arange(places, dtype=jnp.int32)[:, None] == numbers[None, :]).astype(BF16)

    def by_slots(activations):
        here = onehot(stored_here, forget - first_here)
        slot = onehot(SLOTS, jnp.where(chip == z, rank, -1))
        chosen = lax.dot_general(
            slot, here, (((1,), (1,)), ((), ())), preferred_element_type=F32
        ).astype(BF16)
        picked = jnp.dot(chosen, activations, preferred_element_type=F32).astype(BF16)
        there = lax.dynamic_slice_in_dim(picked, (1 - core) * (features // NC), features // NC, 1)
        mine = lax.dynamic_slice_in_dim(picked, core * (features // NC), features // NC, 1)
        slots = gather(mine + swap(there), "z", NZ)
        order = onehot(NZ * SLOTS, chip * SLOTS + rank)
        return lax.dot_general(
            slots, order, (((0,), (0,)), ((), ())), preferred_element_type=F32
        ).astype(BF16)

    def by_sums(activations):
        here = onehot(stored_here, forget - first_here)
        picked = lax.dot_general(
            activations, here, (((0,), (0,)), ((), ())), preferred_element_type=F32
        ).astype(BF16)
        return gather(scatter_sum(fold_cores(picked), "z", NZ).astype(BF16), "z", NZ)

    return lax.cond(jnp.max(rank) < SLOTS, by_slots, by_sums, activations)


def on_device(inverse, activations, forget):
    x, y = lax.axis_index("x"), lax.axis_index("y")
    z, core = lax.axis_index("z"), lax.axis_index("core")
    wide, narrow = x * NY + y, z * NC + core
    height, width = inverse.shape
    to_columns = column_owner()
    to_rows = [(b, a) for a, b in to_columns]

    half = forgotten_half(activations, forget)
    piece = lax.dynamic_slice_in_dim(half, z * (half.shape[0] // NZ), half.shape[0] // NZ, 0)
    piece_by_columns = lax.ppermute(piece, AXES, to_columns)
    rows_here = lax.all_gather(half, "core", axis=0, tiled=True)

    row_number = wide * height + lax.broadcasted_iota(jnp.int32, inverse.shape, 0)
    col_number = narrow * width + lax.broadcasted_iota(jnp.int32, inverse.shape, 1)
    less_one = inverse - jnp.where(row_number == col_number, 1.0, 0.0).astype(F32)
    part = sum(
        lax.dot_general(term, rows_here, (((0,), (0,)), ((), ())), preferred_element_type=F32)
        for term in exact_pair(less_one)
    )
    change = scatter_sum(part.astype(BF16), ("x", "y"), NX * NY).astype(BF16)
    both = jnp.concatenate([piece_by_columns, change], axis=0)
    both = gather(both, "y", NY).reshape(NY, 2, -1, both.shape[1])
    rows_cols = both[:, 0].reshape(-1, both.shape[3])
    change_cols = both[:, 1].reshape(-1, both.shape[3])

    share = sum(
        lax.dot_general(rows_cols, term, (((0,), (0,)), ((), ())), preferred_element_type=F32)
        for term in (rows_cols, change_cols)
    )
    share = scatter_sum(fold_cores(share * BETA).astype(BF16), "z", NZ)
    share = jnp.sum(gather(share[None], "x", NX), axis=0)

    n = share.shape[0]
    own = (core * NZ + z) * n + lax.broadcasted_iota(jnp.int32, share.shape, 0)
    on_diagonal = own == lax.broadcasted_iota(jnp.int32, share.shape, 1)
    high, low = exact_pair(share)
    low = jnp.sum(jnp.where(on_diagonal, low.astype(F32), 0.0), axis=0, keepdims=True)
    low = jnp.pad(low, ((0, PAD - 1), (0, 0))).astype(BF16)
    change_there = lax.ppermute(change, AXES, to_rows)
    gathered = gather(jnp.concatenate([high, low, change_there], axis=0), "z", NZ)
    mine, other = gathered, swap(gathered)
    first = core == 0
    halves = [jnp.where(first, mine, other), jnp.where(first, other, mine)]
    halves = [h.reshape(NZ, -1, h.shape[1]).astype(F32) for h in halves]
    scaled = jnp.concatenate([h[:, :n].reshape(-1, h.shape[2]) for h in halves], axis=0)
    low = jnp.sum(halves[0][:, n] + halves[1][:, n], axis=0)
    diagonal = lax.broadcasted_iota(jnp.int32, scaled.shape, 0) == lax.broadcasted_iota(
        jnp.int32, scaled.shape, 1
    )
    scaled = scaled + jnp.where(diagonal, low[None], 0.0)
    change_here = [h[:, n + PAD :].reshape(-1, h.shape[2]) for h in halves]
    change_here = jnp.concatenate(change_here, axis=0)
    images_rows = rows_here.astype(F32) + change_here
    images_cols = gather((rows_cols.astype(F32) + change_cols.astype(F32)).astype(BF16), "x", NX)

    solved = solve_rows(images_rows * BETA, scaled)
    return inverse + lax.dot_general(
        solved,
        images_cols.astype(F32),
        (((1,), (1,)), ((), ())),
        precision=lax.Precision.HIGH,
        preferred_element_type=F32,
    )


def solution(mesh):
    devices = np.asarray(mesh.devices).reshape(NX, NY, NZ, NC)
    placed = (P(("x", "y"), ("z", "core")), P(("z", "core"), ("x", "y")), P())
    return jax.shard_map(
        on_device,
        mesh=Mesh(devices, AXES),
        in_specs=placed,
        out_specs=P(("x", "y"), ("z", "core")),
        check_vma=False,
    )
```

```python
import math

import jax
import jax.numpy as jnp
import numpy as np
from jax import lax
from jax.experimental.layout import Layout, with_layout_constraint
from jax.sharding import Mesh
from jax.sharding import PartitionSpec as P


M = 16384
ROWS = 512
BETA = 1.0 / (2.0 * (M + 4.0 * math.sqrt(ROWS * M)))
AXES = ("x", "y", "z", "core")
NX, NY, NZ, NC = 4, 8, 8, 2
F32 = jnp.float32
BF16 = jnp.bfloat16
SMALL = 2.0**-6
MAX_FACTORS = 48
PAD = 8
SLOTS = 96


def spread(x, axis, parts):
    x = x.reshape((parts, x.shape[0] // parts) + x.shape[1:])
    return lax.all_to_all(x, axis, 0, 0, tiled=True)


def scatter_sum(x, axis, parts):
    return jnp.sum(spread(x, axis, parts).astype(F32), axis=0)


def gather(x, axis, parts):
    got = lax.all_to_all(jnp.broadcast_to(x[None], (parts,) + x.shape), axis, 0, 0, tiled=True)
    return got.reshape((parts * x.shape[0],) + x.shape[1:])


def swap(x):
    return lax.ppermute(x, "core", [(0, 1), (1, 0)])


def fold_cores(x):
    core = lax.axis_index("core")
    half = x.shape[0] // 2
    there = lax.dynamic_slice_in_dim(x, (1 - core) * half, half, 0)
    here = lax.dynamic_slice_in_dim(x, core * half, half, 0)
    return here + swap(there)


def exact_pair(x):
    high = lax.reduce_precision(x, 8, 7)
    return high.astype(BF16), (x - high).astype(BF16)


def column_owner():
    pairs = []
    for x in range(NX):
        for y in range(NY):
            for z in range(NZ):
                for core in range(NC):
                    here = ((x * NY + y) * NZ + z) * NC + core
                    to_x, to_y = 2 * (y % 2) + core, z
                    to_z, to_core = 2 * x + y // 4, (y // 2) % 2
                    pairs.append((here, ((to_x * NY + to_y) * NZ + to_z) * NC + to_core))
    return pairs


def solve_rows(start, square):
    def dot(a, b, precision=lax.Precision.HIGH):
        return jnp.dot(a, b, precision=precision, preferred_element_type=F32)

    def norm(power):
        return jnp.max(jnp.sum(jnp.abs(power), axis=0))

    def more(state):
        return jnp.logical_and(state[2] > SMALL, state[3] < MAX_FACTORS)

    def step(state):
        total, power, _, count = state
        power = dot(power, power)
        total = with_layout_constraint(total + dot(total, power), Layout((0, 1)))
        return total, power, norm(power), count + 1

    total, power = start + dot(start, square), square
    for _ in range(3):
        power = dot(power, power)
        total = total + dot(total, power)
    total, power, _, _ = lax.while_loop(more, step, (total, power, norm(power), jnp.int32(0)))
    power = dot(power, power, lax.Precision.DEFAULT)
    total = total + dot(total, power, lax.Precision.DEFAULT)
    return total


def forgotten_half(activations, forget):
    z, core = lax.axis_index("z"), lax.axis_index("core")
    stored_here, features = activations.shape
    rows = forget.shape[0]
    first_here = (z * NC + core) * stored_here
    chip = forget // (NC * stored_here)

    earlier = lax.broadcasted_iota(jnp.int32, (rows, rows), 0) < lax.broadcasted_iota(
        jnp.int32, (rows, rows), 1
    )
    rank = jnp.sum((earlier & (chip[:, None] == chip[None, :])).astype(jnp.int32), axis=0)

    def onehot(places, numbers):
        return (jnp.arange(places, dtype=jnp.int32)[:, None] == numbers[None, :]).astype(BF16)

    def by_slots(activations):
        here = onehot(stored_here, forget - first_here)
        slot = onehot(SLOTS, jnp.where(chip == z, rank, -1))
        chosen = lax.dot_general(
            slot, here, (((1,), (1,)), ((), ())), preferred_element_type=F32
        ).astype(BF16)
        picked = jnp.dot(chosen, activations, preferred_element_type=F32).astype(BF16)
        there = lax.dynamic_slice_in_dim(picked, (1 - core) * (features // NC), features // NC, 1)
        mine = lax.dynamic_slice_in_dim(picked, core * (features // NC), features // NC, 1)
        slots = gather(mine + swap(there), "z", NZ)
        order = onehot(NZ * SLOTS, chip * SLOTS + rank)
        return lax.dot_general(
            slots, order, (((0,), (0,)), ((), ())), preferred_element_type=F32
        ).astype(BF16)

    def by_sums(activations):
        here = onehot(stored_here, forget - first_here)
        picked = lax.dot_general(
            activations, here, (((0,), (0,)), ((), ())), preferred_element_type=F32
        ).astype(BF16)
        return gather(scatter_sum(fold_cores(picked), "z", NZ).astype(BF16), "z", NZ)

    return lax.cond(jnp.max(rank) < SLOTS, by_slots, by_sums, activations)


def on_device(inverse, activations, forget):
    x, y = lax.axis_index("x"), lax.axis_index("y")
    z, core = lax.axis_index("z"), lax.axis_index("core")
    wide, narrow = x * NY + y, z * NC + core
    height, width = inverse.shape
    to_columns = column_owner()
    to_rows = [(b, a) for a, b in to_columns]

    half = forgotten_half(activations, forget)
    piece = lax.dynamic_slice_in_dim(half, z * (half.shape[0] // NZ), half.shape[0] // NZ, 0)
    piece_by_columns = lax.ppermute(piece, AXES, to_columns)
    rows_here = lax.all_gather(half, "core", axis=0, tiled=True)

    row_number = wide * height + lax.broadcasted_iota(jnp.int32, inverse.shape, 0)
    col_number = narrow * width + lax.broadcasted_iota(jnp.int32, inverse.shape, 1)
    less_one = inverse - jnp.where(row_number == col_number, 1.0, 0.0).astype(F32)
    part = sum(
        lax.dot_general(term, rows_here, (((0,), (0,)), ((), ())), preferred_element_type=F32)
        for term in exact_pair(less_one)
    ).astype(BF16)
    change = scatter_sum(part, ("x", "y"), NX * NY).astype(BF16)
    both = jnp.concatenate([piece_by_columns, change], axis=0)
    both = gather(both, "y", NY).reshape(NY, 2, -1, both.shape[1])
    rows_cols = both[:, 0].reshape(-1, both.shape[3])
    change_cols = both[:, 1].reshape(-1, both.shape[3])

    share = sum(
        lax.dot_general(rows_cols, term, (((0,), (0,)), ((), ())), preferred_element_type=F32)
        for term in (rows_cols, change_cols)
    )
    share = scatter_sum(fold_cores(share * BETA).astype(BF16), "z", NZ)
    share = jnp.sum(gather(share[None], "x", NX), axis=0)

    n = share.shape[0]
    own = (core * NZ + z) * n + lax.broadcasted_iota(jnp.int32, share.shape, 0)
    on_diagonal = own == lax.broadcasted_iota(jnp.int32, share.shape, 1)
    high, low = exact_pair(share)
    low = jnp.sum(jnp.where(on_diagonal, low.astype(F32), 0.0), axis=0, keepdims=True)
    low = jnp.pad(low, ((0, PAD - 1), (0, 0))).astype(BF16)
    change_there = lax.ppermute(change, AXES, to_rows)
    sent = jnp.concatenate([high, low, change_there], axis=0)
    images = (rows_cols.astype(F32) + change_cols.astype(F32)).astype(BF16)
    images = jnp.broadcast_to(images[None], (NX,) + images.shape)
    sent, images = lax.optimization_barrier((sent, images))
    gathered = gather(sent, "z", NZ)
    images_cols = lax.all_to_all(images, "x", 0, 0, tiled=True).reshape(-1, images.shape[2])
    mine, other = gathered, swap(gathered)
    first = core == 0
    halves = [jnp.where(first, mine, other), jnp.where(first, other, mine)]
    halves = [h.reshape(NZ, -1, h.shape[1]).astype(F32) for h in halves]
    scaled = jnp.concatenate([h[:, :n].reshape(-1, h.shape[2]) for h in halves], axis=0)
    low = jnp.sum(halves[0][:, n] + halves[1][:, n], axis=0)
    diagonal = lax.broadcasted_iota(jnp.int32, scaled.shape, 0) == lax.broadcasted_iota(
        jnp.int32, scaled.shape, 1
    )
    scaled = scaled + jnp.where(diagonal, low[None], 0.0)
    change_here = [h[:, n + PAD :].reshape(-1, h.shape[2]) for h in halves]
    change_here = jnp.concatenate(change_here, axis=0)
    images_rows = rows_here.astype(F32) + change_here
    solved = solve_rows(images_rows * BETA, scaled)
    return inverse + lax.dot_general(
        solved,
        images_cols.astype(F32),
        (((1,), (1,)), ((), ())),
        precision=lax.Precision.HIGH,
        preferred_element_type=F32,
    )


def solution(mesh):
    devices = np.asarray(mesh.devices).reshape(NX, NY, NZ, NC)
    placed = (P(("x", "y"), ("z", "core")), P(("z", "core"), ("x", "y")), P())

    return jax.shard_map(
        on_device,
        mesh=Mesh(devices, AXES),
        in_specs=placed,
        out_specs=P(("x", "y"), ("z", "core")),
        check_vma=False,
    )
```

```python
import math

import jax
import jax.numpy as jnp
import numpy as np
from jax import lax
from jax.experimental import pallas as pl
from jax.experimental.layout import Layout, with_layout_constraint
from jax.experimental.pallas import tpu as pltpu
from jax.sharding import Mesh
from jax.sharding import PartitionSpec as P


M = 16384
ROWS = 512
BETA = 1.0 / (2.0 * (M + 4.0 * math.sqrt(ROWS * M)))
AXES = ("x", "y", "z", "core")
NX, NY, NZ, NC = 4, 8, 8, 2
F32 = jnp.float32
BF16 = jnp.bfloat16
SMALL = 2.0**-6
MAX_FACTORS = 48
PAD = 8
SLOTS = 96


def spread(x, axis, parts):
    x = x.reshape((parts, x.shape[0] // parts) + x.shape[1:])
    return lax.all_to_all(x, axis, 0, 0, tiled=True)


def scatter_sum(x, axis, parts):
    return jnp.sum(spread(x, axis, parts).astype(F32), axis=0)


def gather(x, axis, parts):
    got = lax.all_to_all(jnp.broadcast_to(x[None], (parts,) + x.shape), axis, 0, 0, tiled=True)
    return got.reshape((parts * x.shape[0],) + x.shape[1:])


def swap(x):
    return lax.ppermute(x, "core", [(0, 1), (1, 0)])


def fold_cores(x):
    core = lax.axis_index("core")
    half = x.shape[0] // 2
    there = lax.dynamic_slice_in_dim(x, (1 - core) * half, half, 0)
    here = lax.dynamic_slice_in_dim(x, core * half, half, 0)
    return here + swap(there)


def exact_pair(x):
    high = lax.reduce_precision(x, 8, 7)
    return high.astype(BF16), (x - high).astype(BF16)


def column_owner():
    pairs = []
    for x in range(NX):
        for y in range(NY):
            for z in range(NZ):
                for core in range(NC):
                    here = ((x * NY + y) * NZ + z) * NC + core
                    to_x, to_y = 2 * (y % 2) + core, z
                    to_z, to_core = 2 * x + y // 4, (y // 2) % 2
                    pairs.append((here, ((to_x * NY + to_y) * NZ + to_z) * NC + to_core))
    return pairs


def solve_rows(start, square):
    def dot(a, b, precision=lax.Precision.HIGH):
        return jnp.dot(a, b, precision=precision, preferred_element_type=F32)

    def norm(power):
        return jnp.max(jnp.sum(jnp.abs(power), axis=0))

    def more(state):
        return jnp.logical_and(state[2] > SMALL, state[3] < MAX_FACTORS)

    def step(state):
        total, power, _, count = state
        power = dot(power, power)
        total = with_layout_constraint(total + dot(total, power), Layout((0, 1)))
        return total, power, norm(power), count + 1

    total, power = start + dot(start, square), square
    for _ in range(3):
        power = dot(power, power)
        total = total + dot(total, power)
    total, power, _, _ = lax.while_loop(more, step, (total, power, norm(power), jnp.int32(0)))
    power = dot(power, power, lax.Precision.DEFAULT)
    total = total + dot(total, power, lax.Precision.DEFAULT)
    return total


def forgotten_half(activations, forget):
    z, core = lax.axis_index("z"), lax.axis_index("core")
    stored_here, features = activations.shape
    rows = forget.shape[0]
    first_here = (z * NC + core) * stored_here
    chip = forget // (NC * stored_here)

    earlier = lax.broadcasted_iota(jnp.int32, (rows, rows), 0) < lax.broadcasted_iota(
        jnp.int32, (rows, rows), 1
    )
    rank = jnp.sum((earlier & (chip[:, None] == chip[None, :])).astype(jnp.int32), axis=0)

    def onehot(places, numbers):
        return (jnp.arange(places, dtype=jnp.int32)[:, None] == numbers[None, :]).astype(BF16)

    def by_slots(activations):
        here = onehot(stored_here, forget - first_here)
        slot = onehot(SLOTS, jnp.where(chip == z, rank, -1))
        chosen = lax.dot_general(
            slot, here, (((1,), (1,)), ((), ())), preferred_element_type=F32
        ).astype(BF16)
        picked = jnp.dot(chosen, activations, preferred_element_type=F32).astype(BF16)
        there = lax.dynamic_slice_in_dim(picked, (1 - core) * (features // NC), features // NC, 1)
        mine = lax.dynamic_slice_in_dim(picked, core * (features // NC), features // NC, 1)
        slots = gather(mine + swap(there), "z", NZ)
        order = onehot(NZ * SLOTS, chip * SLOTS + rank)
        return lax.dot_general(
            slots, order, (((0,), (0,)), ((), ())), preferred_element_type=F32
        ).astype(BF16)

    def by_sums(activations):
        here = onehot(stored_here, forget - first_here)
        picked = lax.dot_general(
            activations, here, (((0,), (0,)), ((), ())), preferred_element_type=F32
        ).astype(BF16)
        return gather(scatter_sum(fold_cores(picked), "z", NZ).astype(BF16), "z", NZ)

    return lax.cond(jnp.max(rank) < SLOTS, by_slots, by_sums, activations)


def add_product(inverse, solved, images):
    height, width = inverse.shape
    rows = solved.shape[1]
    block = width // 4

    def kernel(inverse_ref, solved_ref, images_ref, out_ref, high_ref, low_ref):
        @pl.when(pl.program_id(0) == 0)
        def _():
            high = solved_ref[...].astype(BF16)
            high_ref[...] = high
            low_ref[...] = (solved_ref[...] - high.astype(F32)).astype(BF16)

        total = inverse_ref[...]
        for term in (low_ref, high_ref):
            total += lax.dot_general(
                term[...], images_ref[...], (((1,), (1,)), ((), ())), preferred_element_type=F32
            )
        out_ref[...] = total

    return pl.pallas_call(
        kernel,
        out_shape=jax.ShapeDtypeStruct(inverse.shape, F32),
        grid=(width // block,),
        in_specs=[
            pl.BlockSpec((height, block), lambda i: (0, i)),
            pl.BlockSpec((height, rows), lambda i: (0, 0)),
            pl.BlockSpec((block, rows), lambda i: (i, 0)),
        ],
        out_specs=pl.BlockSpec((height, block), lambda i: (0, i)),
        scratch_shapes=[pltpu.VMEM((height, rows), BF16), pltpu.VMEM((height, rows), BF16)],
        compiler_params=pltpu.CompilerParams(vmem_limit_bytes=61 << 20),
        cost_estimate=pl.CostEstimate(
            flops=4 * height * width * rows,
            bytes_accessed=8 * height * width + 4 * height * rows + 2 * width * rows,
            transcendentals=0,
        ),
        name="add_product",
    )(inverse, solved, images)


def on_device(inverse, activations, forget):
    x, y = lax.axis_index("x"), lax.axis_index("y")
    z, core = lax.axis_index("z"), lax.axis_index("core")
    wide, narrow = x * NY + y, z * NC + core
    height, width = inverse.shape
    to_columns = column_owner()
    to_rows = [(b, a) for a, b in to_columns]

    half = forgotten_half(activations, forget)
    piece = lax.dynamic_slice_in_dim(half, z * (half.shape[0] // NZ), half.shape[0] // NZ, 0)
    piece_by_columns = lax.ppermute(piece, AXES, to_columns)
    rows_here = lax.all_gather(half, "core", axis=0, tiled=True)

    row_number = wide * height + lax.broadcasted_iota(jnp.int32, inverse.shape, 0)
    col_number = narrow * width + lax.broadcasted_iota(jnp.int32, inverse.shape, 1)
    less_one = inverse - jnp.where(row_number == col_number, 1.0, 0.0).astype(F32)
    part = sum(
        lax.dot_general(term, rows_here, (((0,), (0,)), ((), ())), preferred_element_type=F32)
        for term in exact_pair(less_one)
    ).astype(BF16)
    change = scatter_sum(part, ("x", "y"), NX * NY).astype(BF16)
    both = jnp.concatenate([piece_by_columns, change], axis=0)
    both = gather(both, "y", NY).reshape(NY, 2, -1, both.shape[1])
    rows_cols = both[:, 0].reshape(-1, both.shape[3])
    change_cols = both[:, 1].reshape(-1, both.shape[3])

    share = sum(
        lax.dot_general(rows_cols, term, (((0,), (0,)), ((), ())), preferred_element_type=F32)
        for term in (rows_cols, change_cols)
    )
    share = share * BETA
    side = share.shape[0] // 2
    beside = share[:side, side:]
    parts = [
        jnp.concatenate([share[:side, :side], beside[: side // 2]], axis=0),
        jnp.concatenate([share[side:, side:], beside[side // 2 :]], axis=0),
    ]
    there = jnp.where(core == 0, parts[1], parts[0])
    share = jnp.where(core == 0, parts[0], parts[1]) + swap(there)
    share = scatter_sum(share.astype(BF16), "z", NZ)
    share = jnp.sum(gather(share[None], "x", NX), axis=0)

    n = share.shape[0]
    own = z * n + lax.broadcasted_iota(jnp.int32, share.shape, 0)
    on_diagonal = own == lax.broadcasted_iota(jnp.int32, share.shape, 1)
    high, low = exact_pair(share)
    low = jnp.sum(jnp.where(on_diagonal, low.astype(F32), 0.0), axis=0, keepdims=True)
    low = jnp.pad(low, ((0, PAD - 1), (0, side))).astype(BF16)
    high = jnp.concatenate([high[: n // 2], high[n // 2 :]], axis=1)
    change_there = lax.ppermute(change, AXES, to_rows)
    sent = jnp.concatenate([high, low, change_there], axis=0)
    images = (rows_cols.astype(F32) + change_cols.astype(F32)).astype(BF16)
    images = jnp.broadcast_to(images[None], (NX,) + images.shape)
    sent, images = lax.optimization_barrier((sent, images))
    gathered = gather(sent, "z", NZ)
    images_cols = lax.all_to_all(images, "x", 0, 0, tiled=True).reshape(-1, images.shape[2])
    mine, other = gathered, swap(gathered)
    first = core == 0
    halves = [jnp.where(first, mine, other), jnp.where(first, other, mine)]
    halves = [h.reshape(NZ, -1, h.shape[1]).astype(F32) for h in halves]
    m = n // 2
    blocks = [
        jnp.concatenate([h[:, :m, :side], h[:, :m, side:]], axis=1).reshape(-1, side) for h in halves
    ]
    lows = [jnp.sum(h[:, m, :side], axis=0) for h in halves]
    diagonal = lax.broadcasted_iota(jnp.int32, (side, side), 0) == lax.broadcasted_iota(
        jnp.int32, (side, side), 1
    )
    corners = [b[:side] + jnp.where(diagonal, l[None], 0.0) for b, l in zip(blocks, lows)]
    beside = jnp.concatenate([b[side:] for b in blocks], axis=0)
    scaled = jnp.concatenate(
        [
            jnp.concatenate([corners[0], beside], axis=1),
            jnp.concatenate([beside.T, corners[1]], axis=1),
        ],
        axis=0,
    )
    change_here = [h[:, m + PAD :].reshape(-1, h.shape[2]) for h in halves]
    change_here = jnp.concatenate(change_here, axis=0)
    images_rows = rows_here.astype(F32) + change_here
    solved = solve_rows(images_rows * BETA, scaled)
    return add_product(inverse, solved, images_cols)


def solution(mesh):
    devices = np.asarray(mesh.devices).reshape(NX, NY, NZ, NC)
    placed = (P(("x", "y"), ("z", "core")), P(("z", "core"), ("x", "y")), P())

    return jax.shard_map(
        on_device,
        mesh=Mesh(devices, AXES),
        in_specs=placed,
        out_specs=P(("x", "y"), ("z", "core")),
        check_vma=False,
    )
```

```python
import math

import jax
import jax.numpy as jnp
import numpy as np
from jax import lax
from jax.experimental.layout import Layout, with_layout_constraint
from jax.sharding import Mesh
from jax.sharding import PartitionSpec as P


M = 16384
ROWS = 512
BETA = 1.0 / (2.0 * (M + 4.0 * math.sqrt(ROWS * M)))
AXES = ("x", "y", "z", "core")
NX, NY, NZ, NC = 4, 8, 8, 2
F32 = jnp.float32
BF16 = jnp.bfloat16
SMALL = 2.0**-6
MAX_FACTORS = 48
PAD = 8
SLOTS = 96


def spread(x, axis, parts):
    x = x.reshape((parts, x.shape[0] // parts) + x.shape[1:])
    return lax.all_to_all(x, axis, 0, 0, tiled=True)


def scatter_sum(x, axis, parts):
    return jnp.sum(spread(x, axis, parts).astype(F32), axis=0)


def gather(x, axis, parts):
    got = lax.all_to_all(jnp.broadcast_to(x[None], (parts,) + x.shape), axis, 0, 0, tiled=True)
    return got.reshape((parts * x.shape[0],) + x.shape[1:])


def swap(x):
    return lax.ppermute(x, "core", [(0, 1), (1, 0)])


def fold_cores(x):
    core = lax.axis_index("core")
    half = x.shape[0] // 2
    there = lax.dynamic_slice_in_dim(x, (1 - core) * half, half, 0)
    here = lax.dynamic_slice_in_dim(x, core * half, half, 0)
    return here + swap(there)


def exact_pair(x):
    high = lax.reduce_precision(x, 8, 7)
    return high.astype(BF16), (x - high).astype(BF16)


def column_owner():
    pairs = []
    for x in range(NX):
        for y in range(NY):
            for z in range(NZ):
                for core in range(NC):
                    here = ((x * NY + y) * NZ + z) * NC + core
                    to_x, to_y = 2 * (y % 2) + core, z
                    to_z, to_core = 2 * x + y // 4, (y // 2) % 2
                    pairs.append((here, ((to_x * NY + to_y) * NZ + to_z) * NC + to_core))
    return pairs


def solve_rows(start, square):
    def dot(a, b, precision=lax.Precision.HIGH):
        return jnp.dot(a, b, precision=precision, preferred_element_type=F32)

    def norm(power):
        return jnp.max(jnp.sum(jnp.abs(power), axis=0))

    def more(state):
        return jnp.logical_and(state[2] > SMALL, state[3] < MAX_FACTORS)

    def step(state):
        total, power, _, count = state
        power = dot(power, power)
        total = with_layout_constraint(total + dot(total, power), Layout((0, 1)))
        return total, power, norm(power), count + 1

    total, power = start + dot(start, square), square
    for _ in range(3):
        power = dot(power, power)
        total = total + dot(total, power)
    total, power, _, _ = lax.while_loop(more, step, (total, power, norm(power), jnp.int32(0)))
    power = dot(power, power, lax.Precision.DEFAULT)
    total = total + dot(total, power, lax.Precision.DEFAULT)
    return total


def forgotten_half(activations, forget):
    z, core = lax.axis_index("z"), lax.axis_index("core")
    stored_here, features = activations.shape
    rows = forget.shape[0]
    first_here = (z * NC + core) * stored_here
    chip = forget // (NC * stored_here)

    earlier = lax.broadcasted_iota(jnp.int32, (rows, rows), 0) < lax.broadcasted_iota(
        jnp.int32, (rows, rows), 1
    )
    rank = jnp.sum((earlier & (chip[:, None] == chip[None, :])).astype(jnp.int32), axis=0)

    def onehot(places, numbers):
        return (jnp.arange(places, dtype=jnp.int32)[:, None] == numbers[None, :]).astype(BF16)

    def by_slots(activations):
        here = onehot(stored_here, forget - first_here)
        slot = onehot(SLOTS, jnp.where(chip == z, rank, -1))
        chosen = lax.dot_general(
            slot, here, (((1,), (1,)), ((), ())), preferred_element_type=F32
        ).astype(BF16)
        picked = jnp.dot(chosen, activations, preferred_element_type=F32).astype(BF16)
        there = lax.dynamic_slice_in_dim(picked, (1 - core) * (features // NC), features // NC, 1)
        mine = lax.dynamic_slice_in_dim(picked, core * (features // NC), features // NC, 1)
        slots = gather(mine + swap(there), "z", NZ)
        order = onehot(NZ * SLOTS, chip * SLOTS + rank)
        return lax.dot_general(
            slots, order, (((0,), (0,)), ((), ())), preferred_element_type=F32
        ).astype(BF16)

    def by_sums(activations):
        here = onehot(stored_here, forget - first_here)
        picked = lax.dot_general(
            activations, here, (((0,), (0,)), ((), ())), preferred_element_type=F32
        ).astype(BF16)
        return gather(scatter_sum(fold_cores(picked), "z", NZ).astype(BF16), "z", NZ)

    return lax.cond(jnp.max(rank) < SLOTS, by_slots, by_sums, activations)


def on_device(inverse, activations, forget):
    x, y = lax.axis_index("x"), lax.axis_index("y")
    z, core = lax.axis_index("z"), lax.axis_index("core")
    wide, narrow = x * NY + y, z * NC + core
    height, width = inverse.shape
    to_columns = column_owner()
    to_rows = [(b, a) for a, b in to_columns]

    half = forgotten_half(activations, forget)
    piece = lax.dynamic_slice_in_dim(half, z * (half.shape[0] // NZ), half.shape[0] // NZ, 0)
    piece_by_columns = lax.ppermute(piece, AXES, to_columns)
    rows_here = lax.all_gather(half, "core", axis=0, tiled=True)

    row_number = wide * height + lax.broadcasted_iota(jnp.int32, inverse.shape, 0)
    col_number = narrow * width + lax.broadcasted_iota(jnp.int32, inverse.shape, 1)
    less_one = inverse - jnp.where(row_number == col_number, 1.0, 0.0).astype(F32)
    part = sum(
        lax.dot_general(term, rows_here, (((0,), (0,)), ((), ())), preferred_element_type=F32)
        for term in exact_pair(less_one)
    ).astype(BF16)
    summed = scatter_sum(part, "x", NX).astype(BF16)
    change = scatter_sum(summed, "y", NY).astype(BF16)
    both = jnp.concatenate([piece_by_columns, change], axis=0)
    both = gather(both, "y", NY).reshape(NY, 2, -1, both.shape[1])
    rows_cols = both[:, 0].reshape(-1, both.shape[3])
    change_cols = both[:, 1].reshape(-1, both.shape[3])

    share = sum(
        lax.dot_general(rows_cols, term, (((0,), (0,)), ((), ())), preferred_element_type=F32)
        for term in (rows_cols, change_cols)
    )

    share = share * BETA
    side = share.shape[0] // 2
    beside = share[:side, side:]
    parts = [
        jnp.concatenate([share[:side, :side], beside[: side // 2]], axis=0),
        jnp.concatenate([share[side:, side:], beside[side // 2 :]], axis=0),
    ]
    there = jnp.where(core == 0, parts[1], parts[0])
    share = jnp.where(core == 0, parts[0], parts[1]) + swap(there)
    share = scatter_sum(share.astype(BF16), "z", NZ)
    share = jnp.sum(gather(share[None], "x", NX), axis=0)

    n = share.shape[0]
    own = z * n + lax.broadcasted_iota(jnp.int32, share.shape, 0)
    on_diagonal = own == lax.broadcasted_iota(jnp.int32, share.shape, 1)
    high, low = exact_pair(share)
    low = jnp.sum(jnp.where(on_diagonal, low.astype(F32), 0.0), axis=0, keepdims=True)
    low = jnp.pad(low, ((0, PAD - 1), (0, side))).astype(BF16)
    high = jnp.concatenate([high[: n // 2], high[n // 2 :]], axis=1)
    change_there = lax.ppermute(change, AXES, to_rows)
    sent = jnp.concatenate([high, low, change_there], axis=0)
    images = (rows_cols.astype(F32) + change_cols.astype(F32)).astype(BF16)
    images = jnp.broadcast_to(images[None], (NX,) + images.shape)
    sent, images = lax.optimization_barrier((sent, images))
    gathered = gather(sent, "z", NZ)
    images_cols = lax.all_to_all(images, "x", 0, 0, tiled=True).reshape(-1, images.shape[2])
    mine, other = gathered, swap(gathered)
    first = core == 0
    halves = [jnp.where(first, mine, other), jnp.where(first, other, mine)]
    halves = [h.reshape(NZ, -1, h.shape[1]).astype(F32) for h in halves]
    m = n // 2
    blocks = [
        jnp.concatenate([h[:, :m, :side], h[:, :m, side:]], axis=1).reshape(-1, side) for h in halves
    ]
    lows = [jnp.sum(h[:, m, :side], axis=0) for h in halves]
    diagonal = lax.broadcasted_iota(jnp.int32, (side, side), 0) == lax.broadcasted_iota(
        jnp.int32, (side, side), 1
    )
    corners = [b[:side] + jnp.where(diagonal, l[None], 0.0) for b, l in zip(blocks, lows)]
    beside = jnp.concatenate([b[side:] for b in blocks], axis=0)
    scaled = jnp.concatenate(
        [
            jnp.concatenate([corners[0], beside], axis=1),
            jnp.concatenate([beside.T, corners[1]], axis=1),
        ],
        axis=0,
    )
    change_here = [h[:, m + PAD :].reshape(-1, h.shape[2]) for h in halves]
    change_here = jnp.concatenate(change_here, axis=0)
    images_rows = rows_here.astype(F32) + change_here
    solved = solve_rows(images_rows * BETA, scaled)
    return inverse + lax.dot_general(
        solved,
        images_cols.astype(F32),
        (((1,), (1,)), ((), ())),
        precision=lax.Precision.HIGH,
        preferred_element_type=F32,
    )


def solution(mesh):
    devices = np.asarray(mesh.devices).reshape(NX, NY, NZ, NC)
    placed = (P(("x", "y"), ("z", "core")), P(("z", "core"), ("x", "y")), P())

    return jax.shard_map(
        on_device,
        mesh=Mesh(devices, AXES),
        in_specs=placed,
        out_specs=P(("x", "y"), ("z", "core")),
        check_vma=False,
    )
```
